32 devices in a mesh: tm: 8 (over y, x, core), head: 4 (over z).
Axes of the slice: x: 2, y: 2, z: 4, core: 2. Of those that a mesh axis runs over, the one named last changes fastest.
Arguments:
- inputs: bfloat16 [32768, 1024], P(('tm', 'head')), may hold values from -54 to 54
- weights: bfloat16 [1024, 768], P(('tm', 'head')), may hold values from -0.1875 to 0.1875
- band_lists: int32 [256, 5], P('tm'), may hold values from 0 to 1, as said below
Outputs:
- attended: bfloat16 [32768, 256], P(('tm', 'head'))
The draws below stay inside these ranges and needn't reach their ends.
Inputs may be any that keep to these rules, and one draw needn't show every extreme that they name: band_lists[b, 2] is 1 for every block b.
All inputs are finite; a program needn't handle non-finite values.
Results may differ from the reference program's by a relative error of at most 0.0045.
The reference program's roundings to bfloat16 on the way count: a program that leaves them out, or rounds other values in their place, can miss the bound.
Values may be sent and summed in bfloat16 or wider, within the bound.
A program may use at most 64 MiB of HBM per device.

```python
import jax
import jax.numpy as jnp
from jax import lax

D = 1024
HD = 64
BLK = 128
REACH = 2
HEADS = 4
TOKENS = 32768
NBLK = 256


def draw_inputs(key, part):
    base = jax.random.truncated_normal(key, -4.5, 4.5, (TOKENS, D), jnp.float32)
    return base.astype(jnp.bfloat16)


def draw_band_lists(key, part):
    span = 2 * REACH + 1
    groups = NBLK // 6 + 1
    levels = jax.random.randint(jax.random.fold_in(key, 21), (groups,), 0, 5)
    which = jnp.arange(NBLK, dtype=jnp.int32) // 6
    picks = jax.random.randint(jax.random.fold_in(key, 22), (NBLK, span), 0, 4)
    listed = (picks < levels[which][:, None]).astype(jnp.int32)
    centre = jnp.arange(span, dtype=jnp.int32)[None, :] == REACH
    return jnp.where(centre, 1, listed).astype(jnp.int32)


def shard_levels(stream_key, dims, cuts, least, top_value):
    loudness, own = 1.0, jax.random.fold_in(stream_key, 6)
    for axis_at, blocks in cuts:
        draws = jnp.exp(jax.random.uniform(jax.random.fold_in(own, axis_at), (blocks,), jnp.float32, least / len(cuts), top_value / len(cuts)))
        loudness = loudness * jnp.repeat(draws, dims[axis_at] // blocks).reshape([-1 if axis == axis_at else 1 for axis in range(len(dims))])
    return loudness


def bell_draw(own_key, shape, scale, bound, cuts=(), kind=jnp.bfloat16):
    values = jax.random.normal(own_key, shape, jnp.float32) * scale
    if len(cuts) > 0:
        values = shard_levels(own_key, shape, cuts, -0.22, 0.18) * values
    return jnp.clip(values, min=-bound, max=bound).astype(kind)


def setup_inputs(seed: int = 0) -> dict:
    key_list = jax.random.split(jax.random.key(seed), 4)
    inputs = draw_inputs(jax.random.fold_in(key_list[3], 71), 0)
    weights = bell_draw(key_list[1], (D, HEADS * 3 * HD), D ** -0.5, 0.1875, ((0, 32),))
    band_lists = draw_band_lists(jax.random.fold_in(key_list[3], 71), 0)
    return {"inputs": inputs, "weights": weights, "band_lists": band_lists}


def attend_masked(query, keys, values, valid, block, reach):
    blocks = query.shape[0] // block
    span = 2 * reach + 1
    window_width = query.shape[1]
    key_blocks = keys.reshape(blocks + 2 * reach, block, window_width)
    value_blocks = values.reshape(blocks + 2 * reach, block, window_width)
    banded_keys = jnp.stack([key_blocks[offset:offset + blocks] for offset in range(span)], axis=1)
    banded_values = jnp.stack([value_blocks[offset:offset + blocks] for offset in range(span)], axis=1)
    grouped_heads = query.reshape(blocks, block, window_width)
    attention_scores = jnp.einsum("nxf,nmzf->nxmz", grouped_heads, banded_keys, preferred_element_type=jnp.float32) * (window_width ** -0.5)
    attention_scores = jnp.where(valid[:, None, :, None], attention_scores, -jnp.inf)
    row_max = jnp.max(attention_scores, axis=(2, 3), keepdims=True)
    attention_probs = jnp.exp(attention_scores - row_max)
    total = jnp.sum(attention_probs, axis=(2, 3))
    mixed_values = jnp.einsum("afuv,auvl->afl", attention_probs.astype(jnp.bfloat16), banded_values, preferred_element_type=jnp.float32)
    return (mixed_values / total[:, :, None]).reshape(blocks * block, window_width)


def reference(inputs, weights, band_lists):
    tokens = inputs.shape[0]
    projected = jnp.dot(inputs, weights, preferred_element_type=jnp.float32).astype(jnp.bfloat16)
    split = projected.reshape(tokens, HEADS, 3, HD)
    margin = REACH * BLK
    blocks = tokens // BLK
    query_block = jnp.arange(blocks, dtype=jnp.int32)
    key_block = query_block[:, None] + jnp.arange(2 * REACH + 1, dtype=jnp.int32)[None, :] - REACH
    valid = (band_lists == 1) & (key_block >= 0) & (key_block < blocks)

    def per_head(parts):
        query = parts[:, 0, :]
        keys = jnp.pad(parts[:, 1, :], ((margin, margin), (0, 0)))
        values = jnp.pad(parts[:, 2, :], ((margin, margin), (0, 0)))
        return attend_masked(query, keys, values, valid, BLK, REACH)

    mixed_values = lax.map(per_head, jnp.transpose(split, (1, 0, 2, 3)))
    return jnp.transpose(mixed_values, (1, 0, 2)).reshape(tokens, HEADS * HD).astype(jnp.bfloat16)
```

```python
import functools

import jax
import jax.numpy as jnp
from jax import lax
from jax.experimental import pallas as pl
from jax.experimental.pallas import tpu as pltpu
from jax.sharding import PartitionSpec as P

HD = 64
BLK = 128
REACH = 2
SPAN = 2 * REACH + 1
MARGIN = REACH * BLK
GROUP = 2
MESH = pl.DeviceIdType.MESH


def attend_block(b, g, first, row0, total_blocks, band_ref, q_buf, kv_buf, out_ref):
    lanes = GROUP * HD
    start = pl.multiple_of(b * BLK, BLK)
    rows = pl.ds(start, BLK)
    window = pl.ds(start, SPAN * BLK)
    bias = []
    for o in range(SPAN):
        key_block = first + b + o - REACH
        ok = (band_ref[o, row0 + b] == 1) & (key_block >= 0) & (key_block < total_blocks)
        bias.append(jnp.where(ok, 0.0, -jnp.inf).astype(jnp.float32))
    head_of = lax.broadcasted_iota(jnp.int32, (BLK, lanes), 1) // HD
    here = slice(g * lanes, (g + 1) * lanes)
    q = q_buf[rows, here]
    k = kv_buf[g, window, :lanes]
    v = kv_buf[g, window, lanes:]
    stacked = jnp.concatenate(
        [jnp.where(head_of == h, q, jnp.zeros_like(q)) for h in range(GROUP)], axis=0
    )
    s = lax.dot_general(stacked, k, (((1,), (1,)), ((), ())), preferred_element_type=jnp.float32)
    parts = [s[:, o * BLK : (o + 1) * BLK] + bias[o] for o in range(SPAN)]
    m = jnp.max(functools.reduce(jnp.maximum, parts), axis=1, keepdims=True)
    probs = [jnp.exp(part - m) for part in parts]
    total = jnp.sum(functools.reduce(jnp.add, probs), axis=1, keepdims=True)
    p = jnp.concatenate([x.astype(jnp.bfloat16) for x in probs], axis=1)
    mixed = jnp.dot(p, v, preferred_element_type=jnp.float32)
    num, den = mixed[:BLK], jnp.broadcast_to(total[:BLK], (BLK, lanes))
    for h in range(1, GROUP):
        part = slice(h * BLK, (h + 1) * BLK)
        num = jnp.where(head_of == h, mixed[part], num)
        den = jnp.where(head_of == h, jnp.broadcast_to(total[part], (BLK, lanes)), den)
    out_ref[rows, here] = (num / den).astype(out_ref.dtype)


def kernel(
    tms, nheads, x_hbm, w_hbm, band_hbm, out_ref,
    x_buf, w_ref, w_buf, kv_buf, q_buf, band_ref,
    x_sem, band_sem, w_sem, w_send, w_recv, halo_send, halo_recv,
):
    tm, hd = lax.axis_index("tm"), lax.axis_index("head")
    shard = w_ref.shape[0]
    rows = x_buf.shape[0]
    heads = w_ref.shape[1] // (3 * HD)
    blocks = rows // BLK
    count = tms * nheads

    def owner(t, h):
        return t * nheads + h

    def z_peer(d):
        return lax.rem(hd + d, nheads)

    me = owner(tm, hd)
    nxt, prv = lax.rem(me + 1, count), lax.rem(me + count - 1, count)
    nxt_id = (nxt // nheads, lax.rem(nxt, nheads))
    prv_id = (prv // nheads, lax.rem(prv, nheads))

    def flip(t, bit):
        return t + bit - 2 * bit * lax.rem(t // bit, 2)

    sib, side, front = flip(tm, 1), flip(tm, 2), flip(tm, 4)
    diag = flip(side, 4)

    barrier = pltpu.get_barrier_semaphore()
    for d in range(1, nheads):
        pl.semaphore_signal(barrier, inc=1, device_id=(tm, z_peer(d)), device_id_type=MESH)
    for t in (side, front, diag, sib):
        pl.semaphore_signal(barrier, inc=1, device_id=(t, hd), device_id_type=MESH)

    w_copy = pltpu.make_async_copy(w_hbm, w_ref, w_sem)
    w_copy.start()
    x_copy = pltpu.make_async_copy(x_hbm, x_buf, x_sem)
    x_copy.start()
    band_copy = pltpu.make_async_copy(band_hbm, band_ref, band_sem)
    band_copy.start()

    w_copy.wait()
    w = w_ref[...].astype(jnp.float32)
    groups = heads // GROUP

    def columns(part, hs):
        return [w[:, (3 * h + part) * HD : (3 * h + part + 1) * HD] for h in hs]

    own = pl.ds(pl.multiple_of(me * shard, shard), shard)
    for g in range(groups):
        hs = range(g * GROUP, (g + 1) * GROUP)
        w_buf[g, own, :] = jnp.concatenate(columns(1, hs) + columns(2, hs), axis=1).astype(
            jnp.bfloat16
        )
    w_buf[groups, own, :] = jnp.concatenate(columns(0, range(heads)), axis=1).astype(jnp.bfloat16)
    pl.semaphore_wait(barrier, nheads - 1 + 4)

    sent = [[], [], []]
    direct = (0,)

    def slot(kind, t, h):
        return w_buf.at[kind, pl.ds(pl.multiple_of(owner(t, h) * shard, shard), shard)]

    def send(kind, t, h, device):
        copy = pltpu.make_async_remote_copy(
            src_ref=slot(kind, t, h), dst_ref=slot(kind, t, h),
            send_sem=w_send.at[kind, len(sent[kind])], recv_sem=w_recv.at[kind, owner(t, h)],
            device_id=device, device_id_type=MESH,
        )
        copy.start()
        sent[kind].append(copy)

    def arrived(kind, t, h):
        pltpu.make_async_remote_copy(
            src_ref=slot(kind, t, h), dst_ref=slot(kind, t, h),
            send_sem=x_sem, recv_sem=w_recv.at[kind, owner(t, h)],
            device_id=(sib, hd), device_id_type=MESH,
        ).wait_recv()

    def to_z(kind):
        for d in range(1, nheads):
            send(kind, tm, hd, (tm, z_peer(d)))

    def spread(kind, d):
        for t in (diag, side, front, sib) if kind in direct else (side, front, sib):
            send(kind, tm, z_peer(d), (t, hd))

    def from_z(kind):
        for d in range(1, nheads):
            arrived(kind, tm, z_peer(d))
            spread(kind, d)

    def from_plane(kind):
        for d in range(nheads):
            h = z_peer(d)
            for t, relay, onward in ((side, 0, front), (front, 1, side)):
                arrived(kind, t, h)
                if kind not in direct and d % 2 == relay:
                    send(kind, t, h, (onward, hd))
                send(kind, t, h, (sib, hd))

    def from_diag(kind):
        for d in range(nheads):
            arrived(kind, diag, z_peer(d))
            send(kind, diag, z_peer(d), (sib, hd))

    def from_sib(kind):
        for t in (tm, side, front, diag):
            for d in range(nheads):
                arrived(kind, flip(t, 1), z_peer(d))

    def project_kv(g, start, size):
        kv_buf[g, MARGIN + start : MARGIN + start + size, :] = jnp.dot(
            x_buf[start : start + size, :], w_buf[g], preferred_element_type=jnp.float32
        ).astype(jnp.bfloat16)

    def halo(g, far, up):
        if up:
            src, dst = (rows, 0) if far else (rows + BLK, BLK)
        else:
            src = MARGIN + BLK if far else MARGIN
            dst = src + rows
        at = 2 * far + up
        return pltpu.make_async_remote_copy(
            src_ref=kv_buf.at[g, pl.ds(src, BLK)], dst_ref=kv_buf.at[g, pl.ds(dst, BLK)],
            send_sem=halo_send.at[g, at], recv_sem=halo_recv.at[g, at],
            device_id=nxt_id if up else prv_id, device_id_type=MESH,
        )

    halos = [[[halo(g, far, up) for up in (0, 1)] for far in (0, 1)] for g in range(groups)]

    def trade(g):
        project_kv(g, 0, MARGIN)
        project_kv(g, rows - MARGIN, MARGIN)
        project_kv(g, MARGIN, BLK)
        (near_down, near_up), (far_down, far_up) = halos[g]

        @pl.when(hd == nheads - 1)
        def _():
            for copy in (near_up, far_up, near_down, far_down):
                copy.start()

        @pl.when(hd == 0)
        def _():
            for copy in (near_down, far_down, near_up, far_up):
                copy.start()

        @pl.when((hd > 0) & (hd < nheads - 1))
        def _():
            for copy in (near_down, near_up, far_down, far_up):
                copy.start()

    to_z(0)
    spread(0, 0)
    to_z(1)
    from_z(0)
    to_z(2)
    from_plane(0)
    spread(1, 0)
    from_z(1)
    from_diag(0)
    x_copy.wait()
    from_sib(0)
    trade(0)
    from_plane(1)
    spread(2, 0)
    from_z(2)
    from_diag(1)
    from_sib(1)
    trade(1)
    from_plane(2)
    from_diag(2)
    for g in range(groups):
        project_kv(g, MARGIN + BLK, rows - 2 * MARGIN - BLK)
    from_sib(2)
    for start in range(0, rows, MARGIN):
        q = jnp.dot(
            x_buf[start : start + MARGIN, :], w_buf[groups], preferred_element_type=jnp.float32
        ).astype(jnp.bfloat16)
        q_buf[start : start + MARGIN, :] = q * jnp.bfloat16(HD ** -0.5)
    band_copy.wait()

    args = (me * blocks, hd * blocks, count * blocks, band_ref, q_buf, kv_buf, out_ref)

    @pl.loop(REACH, blocks - REACH)
    def _(b):
        for g in range(groups):
            attend_block(b, g, *args)

    for g in range(groups):
        for far in (0, 1):
            for copy in halos[g][far]:
                copy.wait()
            for b in ((0, blocks - 1) if far else (1, blocks - 2)):
                attend_block(b, g, *args)

    for copy in sent[0] + sent[1] + sent[2]:
        copy.wait_send()


def fused(tms, nheads, inputs, weights, band_lists):
    rows, depth = inputs.shape
    columns = weights.shape[1]
    width = columns // 3
    count = tms * nheads
    sends = nheads - 1 + 3 * nheads + 3 * nheads + nheads
    dma = pltpu.SemaphoreType.DMA
    return pl.pallas_call(
        functools.partial(kernel, tms, nheads),
        out_shape=jax.ShapeDtypeStruct((rows, width), jnp.bfloat16),
        in_specs=[
            pl.BlockSpec(memory_space=pl.ANY),
            pl.BlockSpec(memory_space=pl.ANY),
            pl.BlockSpec(memory_space=pl.ANY),
        ],
        out_specs=pl.BlockSpec(memory_space=pltpu.VMEM),
        scratch_shapes=[
            pltpu.VMEM((rows, depth), jnp.bfloat16),
            pltpu.VMEM(weights.shape, jnp.bfloat16),
            pltpu.VMEM((3, depth, width), jnp.bfloat16),
            pltpu.VMEM((2, rows + 2 * MARGIN, width), jnp.bfloat16),
            pltpu.VMEM((rows, width), jnp.bfloat16),
            pltpu.SMEM(band_lists.shape[::-1], jnp.int32),
            dma,
            dma,
            dma,
            dma((3, sends)),
            dma((3, count)),
            dma((2, 4)),
            dma((2, 4)),
        ],
        compiler_params=pltpu.CompilerParams(collective_id=0, has_side_effects=True, vmem_limit_bytes=16*1024*1024),
    )(*(pltpu.with_memory_space_constraint(a, pltpu.HBM) for a in (inputs, weights, band_lists.T)))


def padded(block, width):
    count = lax.axis_size("tm")
    forward = [(i, i + 1) for i in range(count - 1)]
    backward = [(target, source) for source, target in forward]
    low = lax.ppermute(block[block.shape[0] - width :], "tm", forward)
    high = lax.ppermute(block[:width], "tm", backward)
    return jnp.concatenate([low, block, high], axis=0)


def attend_masked(query, keys, values, valid):
    blocks = query.shape[0] // BLK
    key_blocks = keys.reshape(blocks + 2 * REACH, BLK, HD)
    value_blocks = values.reshape(blocks + 2 * REACH, BLK, HD)
    banded_keys = jnp.stack([key_blocks[o : o + blocks] for o in range(SPAN)], axis=1)
    banded_values = jnp.stack([value_blocks[o : o + blocks] for o in range(SPAN)], axis=1)
    scores = jnp.einsum(
        "nxf,nmzf->nxmz", query.reshape(blocks, BLK, HD), banded_keys,
        preferred_element_type=jnp.float32,
    ) * HD ** (-0.5)
    scores = jnp.where(valid[:, None, :, None], scores, -jnp.inf)
    probs = jnp.exp(scores - jnp.max(scores, axis=(2, 3), keepdims=True))
    total = jnp.sum(probs, axis=(2, 3))
    mixed = jnp.einsum(
        "afuv,auvl->afl", probs.astype(jnp.bfloat16), banded_values,
        preferred_element_type=jnp.float32,
    )
    return (mixed / total[:, :, None]).reshape(blocks * BLK, HD)


def by_head(inputs, weights, band_lists):
    inputs = lax.all_gather(inputs, "head", axis=0, tiled=True)
    rows = inputs.shape[0]
    head_cols = lax.all_to_all(weights, "head", split_axis=1, concat_axis=0, tiled=True)
    projected = jnp.dot(
        inputs, lax.all_gather(head_cols, "tm", axis=0, tiled=True),
        preferred_element_type=jnp.float32,
    ).astype(jnp.bfloat16)
    blocks = rows // BLK
    query_block = lax.axis_index("tm") * blocks + jnp.arange(blocks, dtype=jnp.int32)
    key_block = query_block[:, None] + jnp.arange(SPAN, dtype=jnp.int32)[None, :] - REACH
    valid = (band_lists == 1) & (key_block >= 0) & (key_block < blocks * lax.axis_size("tm"))
    outs = []
    for h in range(head_cols.shape[1] // (3 * HD)):
        q, k, v = (
            projected[:, (3 * h + part) * HD : (3 * h + part + 1) * HD] for part in range(3)
        )
        keyvals = padded(jnp.concatenate([k, v], axis=1), MARGIN)
        outs.append(attend_masked(q, keyvals[:, :HD], keyvals[:, HD:], valid))
    out = jnp.concatenate(outs, axis=1).astype(jnp.bfloat16)
    return lax.all_to_all(out, "head", split_axis=0, concat_axis=1, tiled=True)


def solution(mesh):
    tms, nheads = mesh.shape["tm"], mesh.shape["head"]

    def on_device(inputs, weights, band_lists):
        heads = weights.shape[1] // (3 * HD)
        small = weights.shape[0] % 16 or inputs.shape[0] < 2 * MARGIN + BLK
        if small or heads != 2 * GROUP or inputs.shape[0] % MARGIN or tms != 8:
            return by_head(inputs, weights, band_lists)
        return fused(tms, nheads, inputs, weights, band_lists)

    return jax.shard_map(
        on_device,
        mesh=mesh,
        in_specs=(P(("tm", "head"), None), P(("tm", "head"), None), P("tm", None)),
        out_specs=P(("tm", "head"), None),
        check_vma=False,
    )
```

```python
import functools

import jax
import jax.numpy as jnp
from jax import lax
from jax.experimental import pallas as pl
from jax.experimental.pallas import tpu as pltpu
from jax.sharding import PartitionSpec as P

HD = 64
BLK = 128
REACH = 2
SPAN = 2 * REACH + 1
MARGIN = REACH * BLK
GROUP = 2
MESH = pl.DeviceIdType.MESH


def attend_block(b, g, first, row0, total_blocks, band_ref, q_buf, kv_buf, out_ref):
    lanes = GROUP * HD
    start = pl.multiple_of(b * BLK, BLK)
    rows = pl.ds(start, BLK)
    window = pl.ds(start, SPAN * BLK)
    bias = []
    for o in range(SPAN):
        key_block = first + b + o - REACH
        ok = (band_ref[o, row0 + b] == 1) & (key_block >= 0) & (key_block < total_blocks)
        bias.append(jnp.where(ok, 0.0, -jnp.inf).astype(jnp.float32))
    head_of = lax.broadcasted_iota(jnp.int32, (BLK, lanes), 1) // HD
    here = slice(g * lanes, (g + 1) * lanes)
    q = q_buf[rows, here]
    k = kv_buf[g, window, :lanes]
    v = kv_buf[g, window, lanes:]
    stacked = jnp.concatenate(
        [jnp.where(head_of == h, q, jnp.zeros_like(q)) for h in range(GROUP)], axis=0
    )
    s = lax.dot_general(stacked, k, (((1,), (1,)), ((), ())), preferred_element_type=jnp.float32)
    parts = [s[:, o * BLK : (o + 1) * BLK] + bias[o] for o in range(SPAN)]
    m = jnp.max(functools.reduce(jnp.maximum, parts), axis=1, keepdims=True)
    probs = [jnp.exp(part - m) for part in parts]
    total = jnp.sum(functools.reduce(jnp.add, probs), axis=1, keepdims=True)
    p = jnp.concatenate([x.astype(jnp.bfloat16) for x in probs], axis=1)
    mixed = jnp.dot(p, v, preferred_element_type=jnp.float32)
    num, den = mixed[:BLK], jnp.broadcast_to(total[:BLK], (BLK, lanes))
    for h in range(1, GROUP):
        part = slice(h * BLK, (h + 1) * BLK)
        num = jnp.where(head_of == h, mixed[part], num)
        den = jnp.where(head_of == h, jnp.broadcast_to(total[part], (BLK, lanes)), den)
    out_ref[rows, here] = (num / den).astype(out_ref.dtype)


def kernel(
    tms, nheads, x_hbm, w_hbm, band_hbm, out_ref,
    x_buf, w_ref, w_buf, kv_buf, q_buf, band_ref,
    x_sem, band_sem, w_sem, w_send, w_recv, halo_send, halo_recv,
):
    tm, hd = lax.axis_index("tm"), lax.axis_index("head")
    shard = w_ref.shape[0]
    rows = x_buf.shape[0]
    heads = w_ref.shape[1] // (3 * HD)
    blocks = rows // BLK
    count = tms * nheads

    def owner(t, h):
        return t * nheads + h

    def z_peer(d):
        return lax.rem(hd + d, nheads)

    me = owner(tm, hd)
    nxt, prv = lax.rem(me + 1, count), lax.rem(me + count - 1, count)
    nxt_id = (nxt // nheads, lax.rem(nxt, nheads))
    prv_id = (prv // nheads, lax.rem(prv, nheads))

    def flip(t, bit):
        return t + bit - 2 * bit * lax.rem(t // bit, 2)

    sib, side, front = flip(tm, 1), flip(tm, 2), flip(tm, 4)
    diag = flip(side, 4)

    barrier = pltpu.get_barrier_semaphore()
    for d in range(1, nheads):
        pl.semaphore_signal(barrier, inc=1, device_id=(tm, z_peer(d)), device_id_type=MESH)
    for t in (side, front, diag, sib):
        pl.semaphore_signal(barrier, inc=1, device_id=(t, hd), device_id_type=MESH)

    w_copy = pltpu.make_async_copy(w_hbm, w_ref, w_sem)
    w_copy.start()
    x_copy = pltpu.make_async_copy(x_hbm, x_buf, x_sem)
    x_copy.start()
    band_copy = pltpu.make_async_copy(band_hbm, band_ref, band_sem)
    band_copy.start()

    w_copy.wait()
    w = w_ref[...].astype(jnp.float32)
    groups = heads // GROUP

    def columns(part, hs):
        return [w[:, (3 * h + part) * HD : (3 * h + part + 1) * HD] for h in hs]

    own = pl.ds(pl.multiple_of(me * shard, shard), shard)
    for g in range(groups):
        hs = range(g * GROUP, (g + 1) * GROUP)
        w_buf[g, own, :] = jnp.concatenate(columns(1, hs) + columns(2, hs), axis=1).astype(
            jnp.bfloat16
        )
    w_buf[groups, own, :] = jnp.concatenate(columns(0, range(heads)), axis=1).astype(jnp.bfloat16)
    pl.semaphore_wait(barrier, nheads - 1 + 4)

    sent = [[], [], []]
    direct = (0, 1)

    def slot(kind, t, h):
        return w_buf.at[kind, pl.ds(pl.multiple_of(owner(t, h) * shard, shard), shard)]

    def send(kind, t, h, device):
        copy = pltpu.make_async_remote_copy(
            src_ref=slot(kind, t, h), dst_ref=slot(kind, t, h),
            send_sem=w_send.at[kind, len(sent[kind])], recv_sem=w_recv.at[kind, owner(t, h)],
            device_id=device, device_id_type=MESH,
        )
        copy.start()
        sent[kind].append(copy)

    def arrived(kind, t, h):
        pltpu.make_async_remote_copy(
            src_ref=slot(kind, t, h), dst_ref=slot(kind, t, h),
            send_sem=x_sem, recv_sem=w_recv.at[kind, owner(t, h)],
            device_id=(sib, hd), device_id_type=MESH,
        ).wait_recv()

    def to_z(kind):
        for d in range(1, nheads):
            send(kind, tm, hd, (tm, z_peer(d)))

    def spread(kind, d):
        for t in (diag, side, front, sib) if kind in direct else (side, front, sib):
            send(kind, tm, z_peer(d), (t, hd))

    def from_z(kind):
        for d in range(1, nheads):
            arrived(kind, tm, z_peer(d))
            spread(kind, d)

    def from_plane(kind):
        for d in range(nheads):
            h = z_peer(d)
            for t, relay, onward in ((side, 0, front), (front, 1, side)):
                arrived(kind, t, h)
                if kind not in direct and d % 2 == relay:
                    send(kind, t, h, (onward, hd))
                send(kind, t, h, (sib, hd))

    def from_diag(kind):
        for d in range(nheads):
            arrived(kind, diag, z_peer(d))
            send(kind, diag, z_peer(d), (sib, hd))

    def from_sib(kind):
        for t in (tm, side, front, diag):
            for d in range(nheads):
                arrived(kind, flip(t, 1), z_peer(d))

    def project_kv(g, start, size):
        kv_buf[g, MARGIN + start : MARGIN + start + size, :] = jnp.dot(
            x_buf[start : start + size, :], w_buf[g], preferred_element_type=jnp.float32
        ).astype(jnp.bfloat16)

    def halo(g, far, up):
        if up:
            src, dst = (rows, 0) if far else (rows + BLK, BLK)
        else:
            src = MARGIN + BLK if far else MARGIN
            dst = src + rows
        at = 2 * far + up
        return pltpu.make_async_remote_copy(
            src_ref=kv_buf.at[g, pl.ds(src, BLK)], dst_ref=kv_buf.at[g, pl.ds(dst, BLK)],
            send_sem=halo_send.at[g, at], recv_sem=halo_recv.at[g, at],
            device_id=nxt_id if up else prv_id, device_id_type=MESH,
        )

    halos = [[[halo(g, far, up) for up in (0, 1)] for far in (0, 1)] for g in range(groups)]

    def trade(g):
        project_kv(g, 0, MARGIN)
        project_kv(g, rows - MARGIN, MARGIN)
        (near_down, near_up), (far_down, far_up) = halos[g]

        @pl.when(hd == nheads - 1)
        def _():
            for copy in (near_up, far_up, near_down, far_down):
                copy.start()

        @pl.when(hd == 0)
        def _():
            for copy in (near_down, far_down, near_up, far_up):
                copy.start()

        @pl.when((hd > 0) & (hd < nheads - 1))
        def _():
            for copy in (near_down, near_up, far_down, far_up):
                copy.start()

    for kind in range(3):
        to_z(kind)
        spread(kind, 0)
    for kind in range(3):
        from_z(kind)
    from_plane(0)
    from_diag(0)
    x_copy.wait()
    from_sib(0)
    trade(0)
    from_plane(1)
    from_diag(1)
    from_sib(1)
    trade(1)
    from_plane(2)
    from_diag(2)
    for g in range(groups):
        project_kv(g, MARGIN, rows - 2 * MARGIN)
    from_sib(2)
    for start in range(0, rows, MARGIN):
        q = jnp.dot(
            x_buf[start : start + MARGIN, :], w_buf[groups], preferred_element_type=jnp.float32
        ).astype(jnp.bfloat16)
        q_buf[start : start + MARGIN, :] = q * jnp.bfloat16(HD ** -0.5)
    band_copy.wait()

    args = (me * blocks, hd * blocks, count * blocks, band_ref, q_buf, kv_buf, out_ref)

    @pl.loop(REACH, blocks - REACH)
    def _(b):
        for g in range(groups):
            attend_block(b, g, *args)

    for g in range(groups):
        for far in (0, 1):
            for copy in halos[g][far]:
                copy.wait()
            for b in ((0, blocks - 1) if far else (1, blocks - 2)):
                attend_block(b, g, *args)

    for copy in sent[0] + sent[1] + sent[2]:
        copy.wait_send()


def fused(tms, nheads, inputs, weights, band_lists):
    rows, depth = inputs.shape
    columns = weights.shape[1]
    width = columns // 3
    count = tms * nheads
    sends = nheads - 1 + 3 * nheads + 3 * nheads + nheads
    dma = pltpu.SemaphoreType.DMA
    return pl.pallas_call(
        functools.partial(kernel, tms, nheads),
        out_shape=jax.ShapeDtypeStruct((rows, width), jnp.bfloat16),
        in_specs=[
            pl.BlockSpec(memory_space=pl.ANY),
            pl.BlockSpec(memory_space=pl.ANY),
            pl.BlockSpec(memory_space=pl.ANY),
        ],
        out_specs=pl.BlockSpec(memory_space=pltpu.VMEM),
        scratch_shapes=[
            pltpu.VMEM((rows, depth), jnp.bfloat16),
            pltpu.VMEM(weights.shape, jnp.bfloat16),
            pltpu.VMEM((3, depth, width), jnp.bfloat16),
            pltpu.VMEM((2, rows + 2 * MARGIN, width), jnp.bfloat16),
            pltpu.VMEM((rows, width), jnp.bfloat16),
            pltpu.SMEM(band_lists.shape[::-1], jnp.int32),
            dma,
            dma,
            dma,
            dma((3, sends)),
            dma((3, count)),
            dma((2, 4)),
            dma((2, 4)),
        ],
        compiler_params=pltpu.CompilerParams(collective_id=0, has_side_effects=True, vmem_limit_bytes=16*1024*1024),
    )(*(pltpu.with_memory_space_constraint(a, pltpu.HBM) for a in (inputs, weights, band_lists.T)))


def padded(block, width):
    count = lax.axis_size("tm")
    forward = [(i, i + 1) for i in range(count - 1)]
    backward = [(target, source) for source, target in forward]
    low = lax.ppermute(block[block.shape[0] - width :], "tm", forward)
    high = lax.ppermute(block[:width], "tm", backward)
    return jnp.concatenate([low, block, high], axis=0)


def attend_masked(query, keys, values, valid):
    blocks = query.shape[0] // BLK
    key_blocks = keys.reshape(blocks + 2 * REACH, BLK, HD)
    value_blocks = values.reshape(blocks + 2 * REACH, BLK, HD)
    banded_keys = jnp.stack([key_blocks[o : o + blocks] for o in range(SPAN)], axis=1)
    banded_values = jnp.stack([value_blocks[o : o + blocks] for o in range(SPAN)], axis=1)
    scores = jnp.einsum(
        "nxf,nmzf->nxmz", query.reshape(blocks, BLK, HD), banded_keys,
        preferred_element_type=jnp.float32,
    ) * HD ** (-0.5)
    scores = jnp.where(valid[:, None, :, None], scores, -jnp.inf)
    probs = jnp.exp(scores - jnp.max(scores, axis=(2, 3), keepdims=True))
    total = jnp.sum(probs, axis=(2, 3))
    mixed = jnp.einsum(
        "afuv,auvl->afl", probs.astype(jnp.bfloat16), banded_values,
        preferred_element_type=jnp.float32,
    )
    return (mixed / total[:, :, None]).reshape(blocks * BLK, HD)


def by_head(inputs, weights, band_lists):
    inputs = lax.all_gather(inputs, "head", axis=0, tiled=True)
    rows = inputs.shape[0]
    head_cols = lax.all_to_all(weights, "head", split_axis=1, concat_axis=0, tiled=True)
    projected = jnp.dot(
        inputs, lax.all_gather(head_cols, "tm", axis=0, tiled=True),
        preferred_element_type=jnp.float32,
    ).astype(jnp.bfloat16)
    blocks = rows // BLK
    query_block = lax.axis_index("tm") * blocks + jnp.arange(blocks, dtype=jnp.int32)
    key_block = query_block[:, None] + jnp.arange(SPAN, dtype=jnp.int32)[None, :] - REACH
    valid = (band_lists == 1) & (key_block >= 0) & (key_block < blocks * lax.axis_size("tm"))
    outs = []
    for h in range(head_cols.shape[1] // (3 * HD)):
        q, k, v = (
            projected[:, (3 * h + part) * HD : (3 * h + part + 1) * HD] for part in range(3)
        )
        keyvals = padded(jnp.concatenate([k, v], axis=1), MARGIN)
        outs.append(attend_masked(q, keyvals[:, :HD], keyvals[:, HD:], valid))
    out = jnp.concatenate(outs, axis=1).astype(jnp.bfloat16)
    return lax.all_to_all(out, "head", split_axis=0, concat_axis=1, tiled=True)


def solution(mesh):
    tms, nheads = mesh.shape["tm"], mesh.shape["head"]

    def on_device(inputs, weights, band_lists):
        heads = weights.shape[1] // (3 * HD)
        small = weights.shape[0] % 16 or inputs.shape[0] < 2 * MARGIN + BLK
        if small or heads != 2 * GROUP or inputs.shape[0] % MARGIN or tms != 8:
            return by_head(inputs, weights, band_lists)
        return fused(tms, nheads, inputs, weights, band_lists)

    return jax.shard_map(
        on_device,
        mesh=mesh,
        in_specs=(P(("tm", "head"), None), P(("tm", "head"), None), P("tm", None)),
        out_specs=P(("tm", "head"), None),
        check_vma=False,
    )
```

```python
import functools

import jax
import jax.numpy as jnp
from jax import lax
from jax.experimental import pallas as pl
from jax.experimental.pallas import tpu as pltpu
from jax.sharding import PartitionSpec as P

HD = 64
BLK = 128
REACH = 2
SPAN = 2 * REACH + 1
MARGIN = REACH * BLK
GROUP = 2
MESH = pl.DeviceIdType.MESH


def attend_block(b, g, first, row0, total_blocks, band_ref, q_buf, kv_buf, out_ref):
    lanes = GROUP * HD
    start = pl.multiple_of(b * BLK, BLK)
    rows = pl.ds(start, BLK)
    window = pl.ds(start, SPAN * BLK)
    bias = []
    for o in range(SPAN):
        key_block = first + b + o - REACH
        ok = (band_ref[o, row0 + b] == 1) & (key_block >= 0) & (key_block < total_blocks)
        bias.append(jnp.where(ok, 0.0, -jnp.inf).astype(jnp.float32))
    head_of = lax.broadcasted_iota(jnp.int32, (BLK, lanes), 1) // HD
    here = slice(g * lanes, (g + 1) * lanes)
    q = q_buf[rows, here]
    k = kv_buf[g, window, :lanes]
    v = kv_buf[g, window, lanes:]
    stacked = jnp.concatenate(
        [jnp.where(head_of == h, q, jnp.zeros_like(q)) for h in range(GROUP)], axis=0
    )
    s = lax.dot_general(stacked, k, (((1,), (1,)), ((), ())), preferred_element_type=jnp.float32)
    parts = [s[:, o * BLK : (o + 1) * BLK] + bias[o] for o in range(SPAN)]
    m = jnp.max(functools.reduce(jnp.maximum, parts), axis=1, keepdims=True)
    probs = [jnp.exp(part - m) for part in parts]
    total = jnp.sum(functools.reduce(jnp.add, probs), axis=1, keepdims=True)
    p = jnp.concatenate([x.astype(jnp.bfloat16) for x in probs], axis=1)
    mixed = jnp.dot(p, v, preferred_element_type=jnp.float32)
    num, den = mixed[:BLK], jnp.broadcast_to(total[:BLK], (BLK, lanes))
    for h in range(1, GROUP):
        part = slice(h * BLK, (h + 1) * BLK)
        num = jnp.where(head_of == h, mixed[part], num)
        den = jnp.where(head_of == h, jnp.broadcast_to(total[part], (BLK, lanes)), den)
    out_ref[rows, here] = (num / den).astype(out_ref.dtype)


def kernel(
    tms, nheads, x_hbm, w_hbm, band_hbm, out_ref,
    x_buf, w_ref, w_buf, kv_buf, q_buf, band_ref,
    x_edge, x_sem, band_sem, w_sem, edge_send, edge_recv, w_send, w_recv, halo_send, halo_recv,
):
    tm, hd = lax.axis_index("tm"), lax.axis_index("head")
    shard = w_ref.shape[0]
    rows = x_buf.shape[0]
    heads = w_ref.shape[1] // (3 * HD)
    blocks = rows // BLK
    count = tms * nheads

    def owner(t, h):
        return t * nheads + h

    def z_peer(d):
        return lax.rem(hd + d, nheads)

    me = owner(tm, hd)
    nxt, prv = lax.rem(me + 1, count), lax.rem(me + count - 1, count)
    nxt_id = (nxt // nheads, lax.rem(nxt, nheads))
    prv_id = (prv // nheads, lax.rem(prv, nheads))

    def flip(t, bit):
        return t + bit - 2 * bit * lax.rem(t // bit, 2)

    sib, side, front = flip(tm, 1), flip(tm, 2), flip(tm, 4)
    diag = flip(side, 4)

    barrier = pltpu.get_barrier_semaphore()
    for d in range(1, nheads):
        pl.semaphore_signal(barrier, inc=1, device_id=(tm, z_peer(d)), device_id_type=MESH)
    for t in (side, front, diag, sib):
        pl.semaphore_signal(barrier, inc=1, device_id=(t, hd), device_id_type=MESH)

    w_copy = pltpu.make_async_copy(w_hbm, w_ref, w_sem)
    w_copy.start()
    x_copy = pltpu.make_async_copy(x_hbm, x_buf, x_sem)
    x_copy.start()
    band_copy = pltpu.make_async_copy(band_hbm, band_ref, band_sem)
    band_copy.start()

    w_copy.wait()
    w = w_ref[...].astype(jnp.float32)
    groups = heads // GROUP

    def columns(part, hs):
        return [w[:, (3 * h + part) * HD : (3 * h + part + 1) * HD] for h in hs]

    own = pl.ds(pl.multiple_of(me * shard, shard), shard)
    for g in range(groups):
        hs = range(g * GROUP, (g + 1) * GROUP)
        w_buf[g, own, :] = jnp.concatenate(columns(1, hs) + columns(2, hs), axis=1).astype(
            jnp.bfloat16
        )
    w_buf[groups, own, :] = jnp.concatenate(columns(0, range(heads)), axis=1).astype(jnp.bfloat16)
    pl.semaphore_wait(barrier, nheads - 1 + 4)

    sent = [[], [], []]
    direct = (0, 1)

    def slot(kind, t, h):
        return w_buf.at[kind, pl.ds(pl.multiple_of(owner(t, h) * shard, shard), shard)]

    def send(kind, t, h, device):
        copy = pltpu.make_async_remote_copy(
            src_ref=slot(kind, t, h), dst_ref=slot(kind, t, h),
            send_sem=w_send.at[kind, len(sent[kind])], recv_sem=w_recv.at[kind, owner(t, h)],
            device_id=device, device_id_type=MESH,
        )
        copy.start()
        sent[kind].append(copy)

    def arrived(kind, t, h):
        pltpu.make_async_remote_copy(
            src_ref=slot(kind, t, h), dst_ref=slot(kind, t, h),
            send_sem=x_sem, recv_sem=w_recv.at[kind, owner(t, h)],
            device_id=(sib, hd), device_id_type=MESH,
        ).wait_recv()

    def to_z(kind):
        for d in range(1, nheads):
            send(kind, tm, hd, (tm, z_peer(d)))

    def spread(kind, d):
        for t in (diag, side, front, sib) if kind in direct else (side, front, sib):
            send(kind, tm, z_peer(d), (t, hd))

    def from_z(kind):
        for d in range(1, nheads):
            arrived(kind, tm, z_peer(d))
            spread(kind, d)

    def from_plane(kind):
        for d in range(nheads):
            h = z_peer(d)
            for t, relay, onward in ((side, 0, front), (front, 1, side)):
                arrived(kind, t, h)
                if kind not in direct and d % 2 == relay:
                    send(kind, t, h, (onward, hd))
                send(kind, t, h, (sib, hd))

    def from_diag(kind):
        for d in range(nheads):
            arrived(kind, diag, z_peer(d))
            send(kind, diag, z_peer(d), (sib, hd))

    def from_sib(kind):
        for t in (tm, side, front, diag):
            for d in range(nheads):
                arrived(kind, flip(t, 1), z_peer(d))

    def project_kv(g, start, size):
        kv_buf[g, MARGIN + start : MARGIN + start + size, :] = jnp.dot(
            x_buf[start : start + size, :], w_buf[g], preferred_element_type=jnp.float32
        ).astype(jnp.bfloat16)

    def halo(g, far, up):
        if up:
            src, dst = (rows, 0) if far else (rows + BLK, BLK)
        else:
            src = MARGIN + BLK if far else MARGIN
            dst = src + rows
        at = 2 * far + up
        return pltpu.make_async_remote_copy(
            src_ref=kv_buf.at[g, pl.ds(src, BLK)], dst_ref=kv_buf.at[g, pl.ds(dst, BLK)],
            send_sem=halo_send.at[g, at], recv_sem=halo_recv.at[g, at],
            device_id=nxt_id if up else prv_id, device_id_type=MESH,
        )

    odd, end = lax.rem(tm, 2), hd // (nheads - 1)
    turn_up = (odd == 0) & (hd == nheads - 1)
    turn_down = (odd == 1) & (hd == 0)
    edge_copy = pltpu.make_async_remote_copy(
        src_ref=x_buf.at[pl.ds(pl.multiple_of(BLK + end * (rows - MARGIN - BLK), BLK), BLK)],
        dst_ref=x_edge, send_sem=edge_send, recv_sem=edge_recv,
        device_id=(sib, nheads - 1 - hd), device_id_type=MESH,
    )

    def project_edge():
        at = pl.multiple_of(end * (MARGIN + BLK + rows), BLK)
        for g in range(groups):
            kv_buf[g, pl.ds(at, BLK), :] = jnp.dot(
                x_edge[...], w_buf[g], preferred_element_type=jnp.float32
            ).astype(jnp.bfloat16)

    halos = [[[halo(g, far, up) for up in (0, 1)] for far in (0, 1)] for g in range(groups)]

    def trade(g):
        project_kv(g, 0, MARGIN)
        project_kv(g, rows - MARGIN, MARGIN)
        (near_down, near_up), (far_down, far_up) = halos[g]

        def begin(*copies):
            for copy in copies:
                copy.start()

        @pl.when(hd == nheads - 1)
        def _():
            begin(near_up)
            pl.when(odd == 1)(far_up.start)
            begin(near_down, far_down)

        @pl.when(hd == 0)
        def _():
            begin(near_down)
            pl.when(odd == 0)(far_down.start)
            begin(near_up, far_up)

        @pl.when((hd > 0) & (hd < nheads - 1))
        def _():
            begin(near_down, near_up, far_down, far_up)

    for kind in range(3):
        to_z(kind)
        spread(kind, 0)
    from_z(0)
    x_copy.wait()
    for kind in range(1, 3):
        from_z(kind)
    pl.when(turn_up | turn_down)(edge_copy.start)
    from_plane(0)
    from_diag(0)
    from_sib(0)
    trade(0)
    from_plane(1)
    from_diag(1)
    from_plane(2)
    from_sib(1)
    trade(1)

    from_diag(2)
    for g in range(groups):
        project_kv(g, MARGIN, rows - 2 * MARGIN)
    from_sib(2)
    for start in range(0, rows, MARGIN):
        q = jnp.dot(
            x_buf[start : start + MARGIN, :], w_buf[groups], preferred_element_type=jnp.float32
        ).astype(jnp.bfloat16)
        q_buf[start : start + MARGIN, :] = q * jnp.bfloat16(HD ** -0.5)
    band_copy.wait()

    args = (me * blocks, hd * blocks, count * blocks, band_ref, q_buf, kv_buf, out_ref)

    @pl.loop(REACH, blocks - REACH)
    def _(b):
        for g in range(groups):
            attend_block(b, g, *args)

    @pl.when(turn_up | turn_down)
    def _():
        edge_copy.wait_recv()
        project_edge()

    for g in range(groups):
        for far in (0, 1):
            down, up = halos[g][far]
            if far:
                pl.when(jnp.logical_not(turn_up))(down.wait_recv)
                pl.when(jnp.logical_not(turn_down))(up.wait_recv)
            else:
                down.wait_recv()
                up.wait_recv()
            for b in ((0, blocks - 1) if far else (1, blocks - 2)):
                attend_block(b, g, *args)

    for g in range(groups):
        (near_down, near_up), (far_down, far_up) = halos[g]
        near_down.wait_send()
        near_up.wait_send()
        pl.when(jnp.logical_not(turn_down))(far_down.wait_send)
        pl.when(jnp.logical_not(turn_up))(far_up.wait_send)
    pl.when(turn_up | turn_down)(edge_copy.wait_send)
    for copy in sent[0] + sent[1] + sent[2]:
        copy.wait_send()


def fused(tms, nheads, inputs, weights, band_lists):
    rows, depth = inputs.shape
    columns = weights.shape[1]
    width = columns // 3
    count = tms * nheads
    sends = nheads - 1 + 3 * nheads + 3 * nheads + nheads
    dma = pltpu.SemaphoreType.DMA
    return pl.pallas_call(
        functools.partial(kernel, tms, nheads),
        out_shape=jax.ShapeDtypeStruct((rows, width), jnp.bfloat16),
        in_specs=[
            pl.BlockSpec(memory_space=pl.ANY),
            pl.BlockSpec(memory_space=pl.ANY),
            pl.BlockSpec(memory_space=pl.ANY),
        ],
        out_specs=pl.BlockSpec(memory_space=pltpu.VMEM),
        scratch_shapes=[
            pltpu.VMEM((rows, depth), jnp.bfloat16),
            pltpu.VMEM(weights.shape, jnp.bfloat16),
            pltpu.VMEM((3, depth, width), jnp.bfloat16),
            pltpu.VMEM((2, rows + 2 * MARGIN, width), jnp.bfloat16),
            pltpu.VMEM((rows, width), jnp.bfloat16),
            pltpu.SMEM(band_lists.shape[::-1], jnp.int32),
            pltpu.VMEM((BLK, depth), jnp.bfloat16),
            dma,
            dma,
            dma,
            dma,
            dma,
            dma((3, sends)),
            dma((3, count)),
            dma((2, 4)),
            dma((2, 4)),
        ],
        compiler_params=pltpu.CompilerParams(collective_id=0, has_side_effects=True, vmem_limit_bytes=16*1024*1024),
    )(*(pltpu.with_memory_space_constraint(a, pltpu.HBM) for a in (inputs, weights, band_lists.T)))


def padded(block, width):
    count = lax.axis_size("tm")
    forward = [(i, i + 1) for i in range(count - 1)]
    backward = [(target, source) for source, target in forward]
    low = lax.ppermute(block[block.shape[0] - width :], "tm", forward)
    high = lax.ppermute(block[:width], "tm", backward)
    return jnp.concatenate([low, block, high], axis=0)


def attend_masked(query, keys, values, valid):
    blocks = query.shape[0] // BLK
    key_blocks = keys.reshape(blocks + 2 * REACH, BLK, HD)
    value_blocks = values.reshape(blocks + 2 * REACH, BLK, HD)
    banded_keys = jnp.stack([key_blocks[o : o + blocks] for o in range(SPAN)], axis=1)
    banded_values = jnp.stack([value_blocks[o : o + blocks] for o in range(SPAN)], axis=1)
    scores = jnp.einsum(
        "nxf,nmzf->nxmz", query.reshape(blocks, BLK, HD), banded_keys,
        preferred_element_type=jnp.float32,
    ) * HD ** (-0.5)
    scores = jnp.where(valid[:, None, :, None], scores, -jnp.inf)
    probs = jnp.exp(scores - jnp.max(scores, axis=(2, 3), keepdims=True))
    total = jnp.sum(probs, axis=(2, 3))
    mixed = jnp.einsum(
        "afuv,auvl->afl", probs.astype(jnp.bfloat16), banded_values,
        preferred_element_type=jnp.float32,
    )
    return (mixed / total[:, :, None]).reshape(blocks * BLK, HD)


def by_head(inputs, weights, band_lists):
    inputs = lax.all_gather(inputs, "head", axis=0, tiled=True)
    rows = inputs.shape[0]
    head_cols = lax.all_to_all(weights, "head", split_axis=1, concat_axis=0, tiled=True)
    projected = jnp.dot(
        inputs, lax.all_gather(head_cols, "tm", axis=0, tiled=True),
        preferred_element_type=jnp.float32,
    ).astype(jnp.bfloat16)
    blocks = rows // BLK
    query_block = lax.axis_index("tm") * blocks + jnp.arange(blocks, dtype=jnp.int32)
    key_block = query_block[:, None] + jnp.arange(SPAN, dtype=jnp.int32)[None, :] - REACH
    valid = (band_lists == 1) & (key_block >= 0) & (key_block < blocks * lax.axis_size("tm"))
    outs = []
    for h in range(head_cols.shape[1] // (3 * HD)):
        q, k, v = (
            projected[:, (3 * h + part) * HD : (3 * h + part + 1) * HD] for part in range(3)
        )
        keyvals = padded(jnp.concatenate([k, v], axis=1), MARGIN)
        outs.append(attend_masked(q, keyvals[:, :HD], keyvals[:, HD:], valid))
    out = jnp.concatenate(outs, axis=1).astype(jnp.bfloat16)
    return lax.all_to_all(out, "head", split_axis=0, concat_axis=1, tiled=True)


def solution(mesh):
    tms, nheads = mesh.shape["tm"], mesh.shape["head"]

    def on_device(inputs, weights, band_lists):
        heads = weights.shape[1] // (3 * HD)
        small = weights.shape[0] % 16 or inputs.shape[0] < 2 * MARGIN + BLK
        if small or heads != 2 * GROUP or inputs.shape[0] % MARGIN or tms != 8 or nheads < 2:
            return by_head(inputs, weights, band_lists)
        return fused(tms, nheads, inputs, weights, band_lists)

    return jax.shard_map(
        on_device,
        mesh=mesh,
        in_specs=(P(("tm", "head"), None), P(("tm", "head"), None), P("tm", None)),
        out_specs=P(("tm", "head"), None),
        check_vma=False,
    )
```
